32 devices in a mesh: row: 8 (over z, x), col: 4 (over y, core).
Axes of the slice: x: 2, y: 2, z: 4, core: 2. Of those that a mesh axis runs over, the one named last changes fastest.
Arguments:
- panels_t: float32 [1024, 2048], P('col', 'row'), as said below
- trailing_t: float32 [3072, 2048], P('col', 'row'), may hold values from -0.125 to 0.125
Outputs:
- r_factor: float32 [1024, 1024], P('row', 'col')
- coefficients: float32 [1024, 3072], P('row', 'col')
The draws below stay inside these ranges and needn't reach their ends.
Inputs may be any that keep to these rules, and one draw needn't show every extreme that they name: `panels_t`: panel_matrix has full column rank.
All inputs are finite; a program needn't handle non-finite values.
Results may differ from the reference program's by a relative error of at most 0.0003.
Values sent between devices are 32-bit elements; how exact they have to be, the bound alone decides.
A program may use at most 64 MiB of HBM per device.

```python
import jax
import jax.numpy as jnp
from jax import lax

TRAIL_COLS = 3072
PANEL_COLS = 1024
ROWS = 2048


def draw_panels_t(key, part):
    key_base = jax.random.fold_in(key, 11)
    key_noise = jax.random.fold_in(key_base, 1)
    key_upper = jax.random.fold_in(key_base, 2)
    key_chain = jax.random.fold_in(key_base, 4)
    key_flip = jax.random.fold_in(key_base, 5)
    noise = jnp.clip(jax.random.normal(key_noise, (PANEL_COLS, ROWS), jnp.float32), -6.0, 6.0)
    noise = noise * ROWS ** (-0.5)
    upper_part = jax.random.normal(key_upper, (PANEL_COLS, PANEL_COLS), jnp.float32) * (0.25 * PANEL_COLS ** (-0.5))
    magnitude = jax.random.uniform(key_chain, (PANEL_COLS - 1,), jnp.float32, 0.8, 0.9)
    flips = jnp.where(jax.random.bernoulli(key_flip, 0.5, (PANEL_COLS - 1,)), 1.0, -1.0).astype(jnp.float32)
    chain = jnp.diag(magnitude * flips, 1)
    upper_part = jnp.triu(upper_part, 1) + chain + jnp.eye(PANEL_COLS, dtype=jnp.float32)
    result = jnp.dot(upper_part.T, noise, precision=lax.Precision.HIGHEST)
    return result


def steps_of(key, extent, shards, low, high):
    level = 1.0
    for dim, parts in shards:
        heights = jax.random.uniform(jax.random.fold_in(jax.random.fold_in(key, 6), dim), (parts,), jnp.float32, low / len(shards), high / len(shards))
        level = level * jnp.repeat(jnp.exp(heights), extent[dim] // parts).reshape((-1,) + (1,) * (len(extent) - 1 - dim))
    return level


def scatter_about(own_key, extent, width, reach, split=(), kind=jnp.bfloat16):
    gain = steps_of(own_key, extent, split, -0.22, 0.18) if split else 1.0
    entries = jax.random.normal(own_key, extent, jnp.float32) * width * gain
    return jnp.minimum(jnp.maximum(entries, -reach), reach).astype(kind)


def setup_inputs(seed: int = 0) -> dict:
    key_of = jax.random.split(jax.random.key(seed), 3)
    panels_t = draw_panels_t(jax.random.fold_in(key_of[2], 71), 0)
    trailing_t = scatter_about(key_of[1], (TRAIL_COLS, ROWS), ROWS ** -0.5, 0.125, ((0, 4), (1, 8)), jnp.float32)
    return {"panels_t": panels_t, "trailing_t": trailing_t}


def reference(panels_t, trailing_t):
    highest = lax.Precision.HIGHEST
    factor_q, raw_r = jnp.linalg.qr(panels_t.T)
    signs = jnp.sign(jnp.diagonal(raw_r))
    r_factor = signs[:, None] * raw_r
    top = signs[:, None] * jnp.dot(factor_q.T, trailing_t.T, precision=highest)
    coefficients = jax.scipy.linalg.solve_triangular(r_factor, top, lower=False)
    return (r_factor, coefficients)
```

```python
import jax
import jax.numpy as jnp
from jax import lax
from jax.experimental import pallas as pl
from jax.experimental.pallas import tpu as pltpu
from jax.sharding import PartitionSpec as P

BLOCK = 128
MICRO = 8
LATE = 1
MESH = pl.DeviceIdType.MESH


def product(left, right):
    return jnp.dot(left, right, precision=lax.Precision.HIGHEST)


def contract(left, right, left_dim, right_dim):
    return lax.dot_general(
        left,
        right,
        (((left_dim,), (right_dim,)), ((), ())),
        precision=lax.Precision.HIGHEST,
        preferred_element_type=jnp.float32,
    )


def lanes(tile, lane):
    return jnp.broadcast_to(tile[:, lane : lane + 1], tile.shape)


def sublanes(tile, row):
    return jnp.broadcast_to(tile[row : row + 1, :], tile.shape)


def factor_block(square):
    count = BLOCK // MICRO
    shape = (MICRO, BLOCK)
    row_id = lax.broadcasted_iota(jnp.int32, shape, 0)
    lane_id = lax.broadcasted_iota(jnp.int32, shape, 1)
    rest = [square[MICRO * i : MICRO * (i + 1), :] for i in range(count)]
    unit = [jnp.where(row_id + MICRO * i == lane_id, 1.0, 0.0) for i in range(count)]
    cols = [lanes(rest[0], c) for c in range(MICRO)]
    upper, inverse = [], []
    for b in range(count):
        base = MICRO * b
        tile, side = rest[b], unit[b]
        scales, pivots, rows, sides = [], {}, [], []
        upper_tile, side_tile = jnp.zeros(shape, jnp.float32), jnp.zeros(shape, jnp.float32)
        for k in range(MICRO):
            scale = lax.rsqrt(sublanes(cols[k], k))
            below = cols[k] * scale
            row = sublanes(tile, k) * scale
            side_row = sublanes(side, k) * scale
            for c in range(k + 1, MICRO):
                pivots[c, k] = sublanes(below, c)
                cols[c] = cols[c] - below * pivots[c, k]
            tile = tile - below * row
            side = side - below * side_row
            upper_tile = jnp.where(row_id == k, row, upper_tile)
            side_tile = jnp.where(row_id == k, side_row, side_tile)
            scales.append(scale)
            rows.append(row)
            sides.append(side_row)
        upper.append(jnp.where(row_id + base <= lane_id, upper_tile, 0.0))
        inverse.append(jnp.where(row_id + base >= lane_id, side_tile, 0.0))
        following = []
        for i in range(b + 1, count):
            tile, side = rest[i], unit[i]
            cols = [lanes(tile, base + c) for c in range(MICRO)]
            ahead = [lanes(tile, base + MICRO + c) for c in range(MICRO)] if i == b + 1 else []
            for k in range(MICRO):
                below = cols[k] * scales[k]
                for c in range(k + 1, MICRO):
                    cols[c] = cols[c] - below * pivots[c, k]
                for c in range(len(ahead)):
                    ahead[c] = ahead[c] - below * sublanes(below, c)
                tile = tile - below * rows[k]
                side = side - below * sides[k]
            rest[i], unit[i] = tile, side
            following = ahead or following
        cols = following
    return jnp.concatenate(upper, axis=0), jnp.concatenate(inverse, axis=0)


def factor_loop(upper_ref, inverse_ref, work_ref, beside):
    total = work_ref.shape[0]
    column = lax.broadcasted_iota(jnp.int32, (BLOCK, total), 1)

    @pl.loop(0, total // BLOCK)
    def _(k):
        start = pl.multiple_of(k * BLOCK, BLOCK)
        here = pl.ds(start, BLOCK)
        diagonal, inverse = factor_block(work_ref[here, here])
        beside(k)
        panel = product(inverse, work_ref[here, :])
        work_ref[here, :] = panel
        work_ref[here, here] = inverse
        upper_ref[here, :] = jnp.where(column >= start + BLOCK, panel, 0.0)
        upper_ref[here, here] = diagonal
        inverse_ref[here, :] = jnp.where(column < start, panel, 0.0)
        inverse_ref[here, here] = inverse

        @pl.loop(k + 1, total // BLOCK)
        def _(i):
            there = pl.ds(pl.multiple_of(i * BLOCK, BLOCK), BLOCK)
            work_ref[there, here] = jnp.zeros((BLOCK, BLOCK), jnp.float32)
            work_ref[there, :] -= contract(work_ref[here, there], work_ref[here, :], 0, 0)


def factor_kernel(gram_ref, upper_ref, inverse_ref, work_ref):
    work_ref[...] = gram_ref[...]
    factor_loop(upper_ref, inverse_ref, work_ref, lambda k: None)


def factor(gram):
    total = gram.shape[0]
    whole = jax.ShapeDtypeStruct((total, total), jnp.float32)
    return pl.pallas_call(
        factor_kernel,
        out_shape=(whole, whole),
        in_specs=[pl.BlockSpec(memory_space=pltpu.VMEM)],
        out_specs=(pl.BlockSpec(memory_space=pltpu.VMEM),) * 2,
        scratch_shapes=[pltpu.VMEM((total, total), jnp.float32)],
        compiler_params=pltpu.CompilerParams(vmem_limit_bytes=32 * 1024 * 1024),
        cost_estimate=pl.CostEstimate(flops=60 * total**3, bytes_accessed=12 * total**2, transcendentals=0),
    )(gram)


def remote(source, target, send, receive, row, col):
    return pltpu.make_async_remote_copy(
        src_ref=source,
        dst_ref=target,
        send_sem=send,
        recv_sem=receive,
        device_id=(row, col),
        device_id_type=MESH,
    )


def greet(peers):
    barrier = pltpu.get_barrier_semaphore()
    for row, col in peers:
        pl.semaphore_signal(barrier, inc=1, device_id=(row, col), device_id_type=MESH)
    pl.semaphore_wait(barrier, len(peers))


def column_peers(cols):
    row, col = lax.axis_index("row"), lax.axis_index("col")
    mate = col + 1 - 2 * lax.rem(col, 2)
    return [(row, lax.rem(col + 2 * t, cols)) for t in range(1, cols // 2)] + [(row, mate)]


def gather_columns(cols, pieces, ready, view, sems):
    line_send, line_recv, mate_send, mate_recv = sems
    row, col = lax.axis_index("row"), lax.axis_index("col")
    mate = col + 1 - 2 * lax.rem(col, 2)
    half = cols // 2
    sent = []

    def launch(copy):
        copy.start()
        sent.append(copy)

    def to_mate(source, owner, s, t):
        launch(remote(source, view(owner, s), mate_send.at[s, t], mate_recv.at[s, t], row, mate))

    def relay(s):
        for t in range(1, half):
            owner = lax.rem(col - 2 * t + cols, cols)
            place = view(owner, s)
            remote(place, place, line_send.at[s, t], line_recv.at[s, t], row, mate).wait_recv()
            to_mate(place, owner, s, t)

    for s in range(pieces):
        source = ready(s)
        for t in range(1, half):
            peer = lax.rem(col + 2 * t, cols)
            launch(remote(source, view(col, s), line_send.at[s, t], line_recv.at[s, t], row, peer))
        to_mate(source, col, s, 0)
        if s > 0:
            relay(s - 1)
    relay(pieces - 1)
    for s in range(pieces):
        for t in range(half):
            place = view(lax.rem(mate - 2 * t + cols, cols), s)
            remote(place, place, mate_send.at[s, t], mate_recv.at[s, t], row, mate).wait_recv()
    for copy in sent:
        copy.wait_send()


def column_sems(cols, pieces):
    return [pltpu.SemaphoreType.DMA((pieces, cols // 2))] * 4


def gather_panel(cols, block_ref, panel_ref, sems):
    pieces = sems[0].shape[0]
    size = block_ref.shape[0] // pieces

    def part(s):
        return pl.ds(s * size, size)

    gather_columns(cols, pieces, lambda s: block_ref.at[part(s)], lambda c, s: panel_ref.at[c, part(s)], sems)
    panel_ref[lax.axis_index("col")] = block_ref[...]


class Reduction:
    def __init__(self, rows, buffer_ref, pair_ref, line_ref, pairs, lines):
        self.buffer, self.pair, self.line = buffer_ref, pair_ref, line_ref
        self.pairs, self.lines = pairs, lines
        self.row, self.col = lax.axis_index("row"), lax.axis_index("col")
        self.half = rows // 2
        self.place, self.side = self.row // 2, lax.rem(self.row, 2)

    def target(self, s, which):
        return 2 * lax.rem(self.place + s, self.half) + which

    def pair_copy(self, s):
        mate = 2 * self.place + 1 - self.side
        source = self.buffer.at[self.target(s, 1 - self.side)]
        return remote(source, self.pair.at[s], self.pairs[0].at[s], self.pairs[1].at[s], mate, self.col)

    def line_copy(self, s):
        owner = self.target(s, self.side)
        source = self.buffer.at[owner]
        return remote(source, self.line.at[s], self.lines[0].at[s], self.lines[1].at[s], owner, self.col)

    def start(self):
        for s in list(range(1, self.half)) + [0]:
            self.pair_copy(s).start()

    def fold(self, s):
        self.pair_copy(s).wait_recv()
        self.buffer[self.target(s, self.side)] += self.pair[s]
        if s > 0:
            self.line_copy(s).start()

    def finish(self):
        self.fold(0)
        total = self.buffer[self.row]
        for s in range(1, self.half):
            self.line_copy(s).wait_recv()
            total = total + self.line[s]
        return total

    def drain(self):
        for s in range(self.half):
            self.pair_copy(s).wait_send()
            if s > 0:
                self.line_copy(s).wait_send()


class Gram:
    STAGES = 7

    def __init__(self, rows, cols, width, panel_ref, buffers, sems):
        self.rows, self.cols, self.width, self.panel = rows, cols, width, panel_ref
        self.buffers, self.sems = buffers, sems
        self.row, self.col = lax.axis_index("row"), lax.axis_index("col")
        self.half, self.across = rows // 2, cols // 2
        self.place, self.side = self.row // 2, lax.rem(self.row, 2)
        self.beside = 2 * self.place + 1 - self.side
        self.mate = self.col + 1 - 2 * lax.rem(self.col, 2)
        self.chunks = gram_chunks(cols)

    def put(self, source, target, which, ch, n, row, col):
        send, receive = self.sems[which]
        copy = remote(source, target, send.at[ch, n], receive.at[ch, n], row, col)
        copy.start()

    def got(self, place, which, ch, n):
        send, receive = self.sems[which]
        remote(place, place, send.at[ch, n], receive.at[ch, n], self.beside, self.col).wait_recv()

    def peer(self, s):
        return lax.rem(self.place + s, self.half)

    def stage(self, ch, st):
        own, first, last = self.chunks[ch]
        part, pair, line, full = self.buffers[ch]
        side, col = self.side, self.col
        thin = self.width // (self.rows * self.cols)
        if st == 0:
            strip = self.panel[own, pl.ds(pl.multiple_of(col * (thin * self.rows), MICRO), thin * self.rows), :]
            right = self.panel[first:last].reshape((last - first) * self.width, -1)
            held = contract(strip, right, 1, 1)
            for r in range(self.rows):
                part[r % 2, r // 2] = held[r * thin : (r + 1) * thin]
            self.put(part.at[1 - side], pair, 0, ch, 0, self.beside, col)
        if st == 1:
            self.got(pair, 0, ch, 0)
            for s in range(self.half):
                part[side, s] += pair[s]
            for s in range(1, self.half):
                to = self.peer(s)
                self.put(part.at[side, to], line.at[s], 1, ch, s, 2 * to + side, col)
        if st == 2:
            total = part[side, self.place]
            for s in range(1, self.half):
                self.got(line.at[s], 1, ch, s)
                total = total + line[s]
            mine = full.at[col, side, self.place]
            full[col, side, self.place] = total
            for s in range(1, self.half):
                self.put(mine, mine, 2, ch, s, 2 * self.peer(s) + side, col)
        if st == 3:
            for s in range(1, self.half):
                self.got(full.at[col, side, self.peer(self.half - s)], 2, ch, s)
            mine = full.at[col, side]
            self.put(mine, mine, 3, ch, 0, self.beside, col)
        if st == 4:
            self.got(full.at[col, 1 - side], 3, ch, 0)
            mine = full.at[col]
            for t in range(1, self.across):
                self.put(mine, mine, 4, ch, t, self.row, lax.rem(col + 2 * t, self.cols))
            self.put(mine, mine, 5, ch, 0, self.row, self.mate)
        if st == 5:
            for t in range(1, self.across):
                place = full.at[lax.rem(col - 2 * t + self.cols, self.cols)]
                self.got(place, 4, ch, t)
                self.put(place, place, 5, ch, t, self.row, self.mate)
        if st == 6:
            for t in range(self.across):
                self.got(full.at[lax.rem(self.mate - 2 * t + self.cols, self.cols)], 5, ch, t)

    def wave(self, w):
        for ch in range(len(self.chunks)):
            if 0 <= w - ch < self.STAGES:
                self.stage(ch, w - ch)

    def place_chunk(self, ch, work_ref, add):
        own, first, last = self.chunks[ch]
        full = self.buffers[ch][3]
        thin = self.width // (self.rows * self.cols)
        columns = pl.ds(first * self.width, (last - first) * self.width)
        for c in range(self.cols):
            for r in range(self.rows):
                there = pl.ds(own * self.width + (c * self.rows + r) * thin, thin)
                held = full[c, r % 2, r // 2]
                work_ref[there, columns] = work_ref[there, columns] + held if add else held

    def drain(self):
        for ch, (part, pair, line, full) in enumerate(self.buffers):
            one, all_places, strip = full.at[0, 0, 0], full.at[0, 0], full.at[0]
            steps = [(0, 0, pair)] + [(1, s, one) for s in range(1, self.half)] + [(2, s, one) for s in range(1, self.half)]
            steps += [(3, 0, all_places)] + [(4, t, strip) for t in range(1, self.across)]
            steps += [(5, t, strip) for t in range(self.across)]
            for which, n, place in steps:
                send, receive = self.sems[which]
                remote(place, place, send.at[ch, n], receive.at[ch, n], self.beside, self.col).wait_send()


def gram_chunks(cols):
    return [(0, 0, 1), (0, 1, cols)] + [(q, q, cols) for q in range(1, cols)]


def solve(cross_ref, inverse_ref, middle_ref, slab_ref):
    total = inverse_ref.shape[0]
    step = 2 * BLOCK
    for j in range(0, total, step):
        stop = j + step
        middle_ref[:, j:stop] = contract(cross_ref[:, :stop], inverse_ref[j:stop, :stop], 1, 1)
    wide = total // slab_ref.shape[0]
    for j in range(0, total, step):
        found = contract(middle_ref[:, j:], inverse_ref[j:, j : j + step], 1, 0)
        for t in range(0, step, wide):
            slab_ref[(j + t) // wide] = found[:, t : t + wide]


def spread_slab(rows, slab_ref, out_ref, send, receive):
    row, col = lax.axis_index("row"), lax.axis_index("col")
    sent = []
    for s in range(1, rows):
        peer = lax.rem(row + s, rows)
        copy = remote(slab_ref.at[peer], out_ref.at[row], send.at[s], receive.at[s], peer, col)
        copy.start()
        sent.append(copy)
    out_ref[row] = slab_ref[row]
    for s in range(1, rows):
        place = out_ref.at[lax.rem(row - s + rows, rows)]
        remote(place, place, send.at[s], receive.at[s], lax.rem(row + s, rows), col).wait_recv()
    for copy in sent:
        copy.wait_send()


def main_kernel(rows, cols, width, *refs):
    block_ref, trailing_ref, upper_out, coef_out, panel_ref = refs[:5]
    cross_ref, pair_ref, line_ref, work_ref, upper_ref, inverse_ref, summed_ref, middle_ref, slab_ref = refs[5:14]
    spreads, pairs, lines = (refs[14 + 2 * i : 16 + 2 * i] for i in range(3))
    first = refs[20:24]
    steps = [refs[24 + 2 * i : 26 + 2 * i] for i in range(6)]
    chunks = gram_chunks(cols)
    buffers = [refs[36 + 4 * i : 40 + 4 * i] for i in range(len(chunks))]
    row, col = lax.axis_index("row"), lax.axis_index("col")
    greet([(lax.rem(row + s, rows), col) for s in range(1, rows)] + column_peers(cols))
    gather_panel(cols, block_ref, panel_ref, first)
    gram = Gram(rows, cols, width, panel_ref, buffers, steps)
    wide = Reduction(rows, cross_ref, pair_ref, line_ref, pairs, lines)
    total = work_ref.shape[0]

    def multiply(begin, end):
        panel = panel_ref[...].reshape(width * cols, panel_ref.shape[2])

        @pl.loop(begin, end)
        def _(r):
            cross_ref[r] = contract(trailing_ref[r], panel, 1, 1)

    ready = Gram.STAGES
    gram.wave(0)
    gram.wave(1)
    work_ref[...] = jnp.zeros_like(work_ref)
    gram.wave(2)
    multiply(0, rows // 2)
    gram.wave(3)
    gram.wave(4)
    multiply(rows // 2, rows)
    gram.wave(5)
    gram.wave(6)
    gram.place_chunk(0, work_ref, False)

    def beside(k):
        for w in range(ready, ready + len(chunks) - 1):
            @pl.when(k == w - ready)
            def _(w=w):
                gram.wave(w)
                gram.place_chunk(w - ready + 1, work_ref, w > ready)
                if w == ready + LATE:
                    wide.start()
        for s in range(1, rows // 2):
            pl.when(k == s + LATE + 1)(lambda s=s: wide.fold(s))

    factor_loop(upper_ref, inverse_ref, work_ref, beside)
    upper_out[...] = upper_ref[
        pl.ds(pl.multiple_of(row * upper_out.shape[0], MICRO), upper_out.shape[0]),
        pl.ds(pl.multiple_of(col * upper_out.shape[1], BLOCK), upper_out.shape[1]),
    ]
    summed_ref[...] = wide.finish()
    solve(summed_ref, inverse_ref, middle_ref, slab_ref)
    spread_slab(rows, slab_ref, coef_out, *spreads)
    wide.drain()
    gram.drain()


def direct(panels_t, trailing_t, rows, cols):
    width, depth = panels_t.shape
    total = width * cols
    half = rows // 2
    trailing = trailing_t.reshape(rows, -1, depth)
    thick = trailing.shape[1]
    thin = width // (rows * cols)
    vmem = pl.BlockSpec(memory_space=pltpu.VMEM)
    shapes = [
        (cols, width, depth),
        (rows, thick, total),
        (half, thick, total),
        (half, thick, total),
        (total, total),
        (total, total),
        (total, total),
        (thick, total),
        (thick, total),
        (rows, thick, total // rows),
    ]
    chunks = gram_chunks(cols)
    staged = []
    for _, begin, end in chunks:
        wide = (end - begin) * width
        staged += [(2, half, thin, wide), (half, thin, wide), (half, thin, wide), (cols, 2, half, thin, wide)]
    semaphores = [pltpu.SemaphoreType.DMA((rows,))] * 2 + [pltpu.SemaphoreType.DMA((half,))] * 4
    steps = [1, half, half, 1, cols // 2, cols // 2]
    stepped = [pltpu.SemaphoreType.DMA((len(chunks), n)) for n in steps for _ in range(2)]
    r_block, spread = pl.pallas_call(
        lambda *refs: main_kernel(rows, cols, width, *refs),
        out_shape=(
            jax.ShapeDtypeStruct((total // rows, total // cols), jnp.float32),
            jax.ShapeDtypeStruct((rows, thick, total // rows), jnp.float32),
        ),
        in_specs=[vmem] * 2,
        out_specs=(vmem, vmem),
        scratch_shapes=[pltpu.VMEM(shape, jnp.float32) for shape in shapes]
        + semaphores
        + column_sems(cols, 2)
        + stepped
        + [pltpu.VMEM(shape, jnp.float32) for shape in staged],
        compiler_params=pltpu.CompilerParams(collective_id=1, has_side_effects=True, vmem_limit_bytes=48 * 1024 * 1024),
    )(panels_t, trailing)
    return r_block, spread.transpose(2, 0, 1).reshape(total // rows, -1)


def plain(panels_t, trailing_t):
    panel = lax.all_gather(panels_t, "col", axis=0, tiled=True)
    gram_part = lax.psum_scatter(product(panels_t, panel.T), "row", scatter_dimension=0, tiled=True)
    gram = lax.all_gather(gram_part, ("col", "row"), axis=0, tiled=True)
    cross = lax.psum_scatter(product(trailing_t, panel.T), "row", scatter_dimension=0, tiled=True)
    r_full, invert = factor(gram)
    slab = product(product(cross, invert.T), invert)
    return r_full, lax.all_to_all(slab, "row", split_axis=1, concat_axis=0, tiled=True).T


def local(panels_t, trailing_t):
    rows, cols = lax.axis_size("row"), lax.axis_size("col")
    width = panels_t.shape[0]
    total = width * cols
    thick = trailing_t.shape[0] // rows
    tiled = width % BLOCK == 0 and total // rows % BLOCK == 0 and width // rows % (cols * MICRO) == 0 and thick % MICRO == 0
    if tiled and rows % 2 == 0 and cols % 2 == 0 and rows // 2 + LATE < total // BLOCK and cols >= 4:
        return direct(panels_t, trailing_t, rows, cols)
    r_full, coef_block = plain(panels_t, trailing_t)
    rows_out = total // rows
    row_start = lax.axis_index("row") * rows_out
    col_start = lax.axis_index("col") * width
    r_block = lax.dynamic_slice(r_full, (row_start, col_start), (rows_out, width))
    return (r_block, coef_block)


def solution(mesh):
    placed = (P("col", "row"), P("col", "row"))
    return jax.shard_map(
        local,
        mesh=mesh,
        in_specs=placed,
        out_specs=(P("row", "col"), P("row", "col")),
        check_vma=False,
    )
```

```python
import jax
import jax.numpy as jnp
from jax import lax
from jax.experimental import pallas as pl
from jax.experimental.pallas import tpu as pltpu
from jax.sharding import PartitionSpec as P

BLOCK = 128
MICRO = 8
LATE = 1
MESH = pl.DeviceIdType.MESH


def product(left, right):
    return jnp.dot(left, right, precision=lax.Precision.HIGHEST)


def contract(left, right, left_dim, right_dim):
    return lax.dot_general(
        left,
        right,
        (((left_dim,), (right_dim,)), ((), ())),
        precision=lax.Precision.HIGHEST,
        preferred_element_type=jnp.float32,
    )


def lanes(tile, lane):
    return jnp.broadcast_to(tile[:, lane : lane + 1], tile.shape)


def sublanes(tile, row):
    return jnp.broadcast_to(tile[row : row + 1, :], tile.shape)


def factor_block(square):
    count = BLOCK // MICRO
    shape = (MICRO, BLOCK)
    row_id = lax.broadcasted_iota(jnp.int32, shape, 0)
    lane_id = lax.broadcasted_iota(jnp.int32, shape, 1)
    rest = [square[MICRO * i : MICRO * (i + 1), :] for i in range(count)]
    unit = [jnp.where(row_id + MICRO * i == lane_id, 1.0, 0.0) for i in range(count)]
    cols = [lanes(rest[0], c) for c in range(MICRO)]
    upper, inverse = [], []
    for b in range(count):
        base = MICRO * b
        tile, side = rest[b], unit[b]
        scales, pivots, rows, sides = [], {}, [], []
        upper_tile, side_tile = jnp.zeros(shape, jnp.float32), jnp.zeros(shape, jnp.float32)
        for k in range(MICRO):
            scale = lax.rsqrt(sublanes(cols[k], k))
            below = cols[k] * scale
            row = sublanes(tile, k) * scale
            side_row = sublanes(side, k) * scale
            for c in range(k + 1, MICRO):
                pivots[c, k] = sublanes(below, c)
                cols[c] = cols[c] - below * pivots[c, k]
            tile = tile - below * row
            side = side - below * side_row
            upper_tile = jnp.where(row_id == k, row, upper_tile)
            side_tile = jnp.where(row_id == k, side_row, side_tile)
            scales.append(scale)
            rows.append(row)
            sides.append(side_row)
        upper.append(jnp.where(row_id + base <= lane_id, upper_tile, 0.0))
        inverse.append(jnp.where(row_id + base >= lane_id, side_tile, 0.0))
        following = []
        for i in range(b + 1, count):
            tile, side = rest[i], unit[i]
            cols = [lanes(tile, base + c) for c in range(MICRO)]
            ahead = [lanes(tile, base + MICRO + c) for c in range(MICRO)] if i == b + 1 else []
            for k in range(MICRO):
                below = cols[k] * scales[k]
                for c in range(k + 1, MICRO):
                    cols[c] = cols[c] - below * pivots[c, k]
                for c in range(len(ahead)):
                    ahead[c] = ahead[c] - below * sublanes(below, c)
                tile = tile - below * rows[k]
                side = side - below * sides[k]
            rest[i], unit[i] = tile, side
            following = ahead or following
        cols = following
    return jnp.concatenate(upper, axis=0), jnp.concatenate(inverse, axis=0)


def factor_loop(upper_ref, inverse_ref, work_ref, beside):
    total = work_ref.shape[0]
    column = lax.broadcasted_iota(jnp.int32, (BLOCK, total), 1)

    @pl.loop(0, total // BLOCK)
    def _(k):
        start = pl.multiple_of(k * BLOCK, BLOCK)
        here = pl.ds(start, BLOCK)
        diagonal, inverse = factor_block(work_ref[here, here])
        beside(k)
        panel = product(inverse, work_ref[here, :])
        work_ref[here, :] = panel
        work_ref[here, here] = inverse
        upper_ref[here, :] = jnp.where(column >= start + BLOCK, panel, 0.0)
        upper_ref[here, here] = diagonal
        inverse_ref[here, :] = jnp.where(column < start, panel, 0.0)
        inverse_ref[here, here] = inverse

        @pl.loop(k + 1, total // BLOCK)
        def _(i):
            there = pl.ds(pl.multiple_of(i * BLOCK, BLOCK), BLOCK)
            work_ref[there, here] = jnp.zeros((BLOCK, BLOCK), jnp.float32)
            work_ref[there, :] -= contract(work_ref[here, there], work_ref[here, :], 0, 0)


def factor_kernel(gram_ref, upper_ref, inverse_ref, work_ref):
    work_ref[...] = gram_ref[...]
    factor_loop(upper_ref, inverse_ref, work_ref, lambda k: None)


def factor(gram):
    total = gram.shape[0]
    whole = jax.ShapeDtypeStruct((total, total), jnp.float32)
    return pl.pallas_call(
        factor_kernel,
        out_shape=(whole, whole),
        in_specs=[pl.BlockSpec(memory_space=pltpu.VMEM)],
        out_specs=(pl.BlockSpec(memory_space=pltpu.VMEM),) * 2,
        scratch_shapes=[pltpu.VMEM((total, total), jnp.float32)],
        compiler_params=pltpu.CompilerParams(vmem_limit_bytes=32 * 1024 * 1024),
        cost_estimate=pl.CostEstimate(flops=60 * total**3, bytes_accessed=12 * total**2, transcendentals=0),
    )(gram)


def remote(source, target, send, receive, row, col):
    return pltpu.make_async_remote_copy(
        src_ref=source,
        dst_ref=target,
        send_sem=send,
        recv_sem=receive,
        device_id=(row, col),
        device_id_type=MESH,
    )


def greet(peers):
    barrier = pltpu.get_barrier_semaphore()
    for row, col in peers:
        pl.semaphore_signal(barrier, inc=1, device_id=(row, col), device_id_type=MESH)
    pl.semaphore_wait(barrier, len(peers))


def column_peers(cols):
    row, col = lax.axis_index("row"), lax.axis_index("col")
    mate = col + 1 - 2 * lax.rem(col, 2)
    return [(row, lax.rem(col + 2 * t, cols)) for t in range(1, cols // 2)] + [(row, mate)]


def gather_columns(cols, pieces, ready, view, sems):
    line_send, line_recv, mate_send, mate_recv = sems
    row, col = lax.axis_index("row"), lax.axis_index("col")
    mate = col + 1 - 2 * lax.rem(col, 2)
    half = cols // 2
    sent = []

    def launch(copy):
        copy.start()
        sent.append(copy)

    def to_mate(source, owner, s, t):
        launch(remote(source, view(owner, s), mate_send.at[s, t], mate_recv.at[s, t], row, mate))

    def relay(s):
        for t in range(1, half):
            owner = lax.rem(col - 2 * t + cols, cols)
            place = view(owner, s)
            remote(place, place, line_send.at[s, t], line_recv.at[s, t], row, mate).wait_recv()
            to_mate(place, owner, s, t)

    for s in range(pieces):
        source = ready(s)
        for t in range(1, half):
            peer = lax.rem(col + 2 * t, cols)
            launch(remote(source, view(col, s), line_send.at[s, t], line_recv.at[s, t], row, peer))
        to_mate(source, col, s, 0)
        if s > 0:
            relay(s - 1)
    relay(pieces - 1)
    for s in range(pieces):
        for t in range(half):
            place = view(lax.rem(mate - 2 * t + cols, cols), s)
            remote(place, place, mate_send.at[s, t], mate_recv.at[s, t], row, mate).wait_recv()
    for copy in sent:
        copy.wait_send()


def column_sems(cols, pieces):
    return [pltpu.SemaphoreType.DMA((pieces, cols // 2))] * 4


def gather_panel(cols, block_ref, panel_ref, sems):
    pieces = sems[0].shape[0]
    size = block_ref.shape[0] // pieces

    def part(s):
        return pl.ds(s * size, size)

    gather_columns(cols, pieces, lambda s: block_ref.at[part(s)], lambda c, s: panel_ref.at[c, part(s)], sems)
    panel_ref[lax.axis_index("col")] = block_ref[...]


class Reduction:
    def __init__(self, rows, buffer_ref, pair_ref, line_ref, pairs, lines):
        self.buffer, self.pair, self.line = buffer_ref, pair_ref, line_ref
        self.pairs, self.lines = pairs, lines
        self.row, self.col = lax.axis_index("row"), lax.axis_index("col")
        self.half = rows // 2
        self.place, self.side = self.row // 2, lax.rem(self.row, 2)

    def target(self, s, which):
        return 2 * lax.rem(self.place + s, self.half) + which

    def pair_copy(self, s):
        mate = 2 * self.place + 1 - self.side
        source = self.buffer.at[self.target(s, 1 - self.side)]
        return remote(source, self.pair.at[s], self.pairs[0].at[s], self.pairs[1].at[s], mate, self.col)

    def line_copy(self, s):
        owner = self.target(s, self.side)
        source = self.buffer.at[owner]
        return remote(source, self.line.at[s], self.lines[0].at[s], self.lines[1].at[s], owner, self.col)

    def start(self, begin, end):
        for s in range(begin, end):
            self.pair_copy(s % self.half).start()

    def fold(self, s):
        self.pair_copy(s).wait_recv()
        self.buffer[self.target(s, self.side)] += self.pair[s]
        if s > 0:
            self.line_copy(s).start()

    def finish(self):
        self.fold(0)
        total = self.buffer[self.row]
        for s in range(1, self.half):
            self.line_copy(s).wait_recv()
            total = total + self.line[s]
        return total

    def drain(self):
        for s in range(self.half):
            self.pair_copy(s).wait_send()
            if s > 0:
                self.line_copy(s).wait_send()


class Gram:
    STAGES = 7

    def __init__(self, rows, cols, width, panel_ref, buffers, sems):
        self.rows, self.cols, self.width, self.panel = rows, cols, width, panel_ref
        self.buffers, self.sems = buffers, sems
        self.row, self.col = lax.axis_index("row"), lax.axis_index("col")
        self.half, self.across = rows // 2, cols // 2
        self.place, self.side = self.row // 2, lax.rem(self.row, 2)
        self.beside = 2 * self.place + 1 - self.side
        self.mate = self.col + 1 - 2 * lax.rem(self.col, 2)
        self.chunks = gram_chunks(cols)

    def put(self, source, target, which, ch, n, row, col):
        send, receive = self.sems[which]
        copy = remote(source, target, send.at[ch, n], receive.at[ch, n], row, col)
        copy.start()

    def got(self, place, which, ch, n):
        send, receive = self.sems[which]
        remote(place, place, send.at[ch, n], receive.at[ch, n], self.beside, self.col).wait_recv()

    def peer(self, s):
        return lax.rem(self.place + s, self.half)

    def stage(self, ch, st):
        own, first, last = self.chunks[ch]
        part, pair, line, full = self.buffers[ch]
        side, col = self.side, self.col
        thin = self.width // (self.rows * self.cols)
        if st == 0:
            strip = self.panel[own, pl.ds(pl.multiple_of(col * (thin * self.rows), MICRO), thin * self.rows), :]
            right = self.panel[first:last].reshape((last - first) * self.width, -1)
            held = contract(strip, right, 1, 1)
            for r in range(self.rows):
                part[r % 2, r // 2] = held[r * thin : (r + 1) * thin]
            self.put(part.at[1 - side], pair, 0, ch, 0, self.beside, col)
        if st == 1:
            self.got(pair, 0, ch, 0)
            for s in range(self.half):
                part[side, s] += pair[s]
            for s in range(1, self.half):
                to = self.peer(s)
                self.put(part.at[side, to], line.at[s], 1, ch, s, 2 * to + side, col)
        if st == 2:
            total = part[side, self.place]
            for s in range(1, self.half):
                self.got(line.at[s], 1, ch, s)
                total = total + line[s]
            mine = full.at[col, side, self.place]
            full[col, side, self.place] = total
            for s in range(1, self.half):
                self.put(mine, mine, 2, ch, s, 2 * self.peer(s) + side, col)
        if st == 3:
            for s in range(1, self.half):
                self.got(full.at[col, side, self.peer(self.half - s)], 2, ch, s)
            mine = full.at[col, side]
            self.put(mine, mine, 3, ch, 0, self.beside, col)
        if st == 4:
            self.got(full.at[col, 1 - side], 3, ch, 0)
            mine = full.at[col]
            for t in range(1, self.across):
                self.put(mine, mine, 4, ch, t, self.row, lax.rem(col + 2 * t, self.cols))
            self.put(mine, mine, 5, ch, 0, self.row, self.mate)
        if st == 5:
            for t in range(1, self.across):
                place = full.at[lax.rem(col - 2 * t + self.cols, self.cols)]
                self.got(place, 4, ch, t)
                self.put(place, place, 5, ch, t, self.row, self.mate)
        if st == 6:
            for t in range(self.across):
                self.got(full.at[lax.rem(self.mate - 2 * t + self.cols, self.cols)], 5, ch, t)

    def wave(self, w):
        for ch in range(len(self.chunks)):
            if 0 <= w - ch < self.STAGES:
                self.stage(ch, w - ch)

    def place_chunk(self, ch, work_ref, add):
        own, first, last = self.chunks[ch]
        full = self.buffers[ch][3]
        thin = self.width // (self.rows * self.cols)
        columns = pl.ds(first * self.width, (last - first) * self.width)
        for c in range(self.cols):
            for r in range(self.rows):
                there = pl.ds(own * self.width + (c * self.rows + r) * thin, thin)
                held = full[c, r % 2, r // 2]
                work_ref[there, columns] = work_ref[there, columns] + held if add else held

    def drain(self):
        for ch, (part, pair, line, full) in enumerate(self.buffers):
            one, all_places, strip = full.at[0, 0, 0], full.at[0, 0], full.at[0]
            steps = [(0, 0, pair)] + [(1, s, one) for s in range(1, self.half)] + [(2, s, one) for s in range(1, self.half)]
            steps += [(3, 0, all_places)] + [(4, t, strip) for t in range(1, self.across)]
            steps += [(5, t, strip) for t in range(self.across)]
            for which, n, place in steps:
                send, receive = self.sems[which]
                remote(place, place, send.at[ch, n], receive.at[ch, n], self.beside, self.col).wait_send()


def gram_chunks(cols):
    return [(0, 0, 1), (0, 1, cols)] + [(q, q, cols) for q in range(1, cols)]


def solve(cross_ref, inverse_ref, middle_ref, slab_ref):
    total = inverse_ref.shape[0]
    step = 2 * BLOCK
    for j in range(0, total, step):
        stop = j + step
        middle_ref[:, j:stop] = contract(cross_ref[:, :stop], inverse_ref[j:stop, :stop], 1, 1)
    wide = total // slab_ref.shape[0]
    for j in range(0, total, step):
        found = contract(middle_ref[:, j:], inverse_ref[j:, j : j + step], 1, 0)
        for t in range(0, step, wide):
            slab_ref[(j + t) // wide] = found[:, t : t + wide]


def spread_slab(rows, slab_ref, out_ref, send, receive):
    row, col = lax.axis_index("row"), lax.axis_index("col")
    sent = []
    for s in range(1, rows):
        peer = lax.rem(row + s, rows)
        copy = remote(slab_ref.at[peer], out_ref.at[row], send.at[s], receive.at[s], peer, col)
        copy.start()
        sent.append(copy)
    out_ref[row] = slab_ref[row]
    for s in range(1, rows):
        place = out_ref.at[lax.rem(row - s + rows, rows)]
        remote(place, place, send.at[s], receive.at[s], lax.rem(row + s, rows), col).wait_recv()
    for copy in sent:
        copy.wait_send()


def main_kernel(rows, cols, width, *refs):
    block_ref, trailing_ref, upper_out, coef_out, panel_ref = refs[:5]
    cross_ref, pair_ref, line_ref, work_ref, upper_ref, inverse_ref, summed_ref, middle_ref, slab_ref = refs[5:14]
    spreads, pairs, lines = (refs[14 + 2 * i : 16 + 2 * i] for i in range(3))
    first = refs[20:24]
    steps = [refs[24 + 2 * i : 26 + 2 * i] for i in range(6)]
    chunks = gram_chunks(cols)
    buffers = [refs[36 + 4 * i : 40 + 4 * i] for i in range(len(chunks))]
    row, col = lax.axis_index("row"), lax.axis_index("col")
    greet([(lax.rem(row + s, rows), col) for s in range(1, rows)] + column_peers(cols))
    gather_panel(cols, block_ref, panel_ref, first)
    gram = Gram(rows, cols, width, panel_ref, buffers, steps)
    wide = Reduction(rows, cross_ref, pair_ref, line_ref, pairs, lines)
    total = work_ref.shape[0]

    def multiply(begin, end):
        panel = panel_ref[...].reshape(width * cols, panel_ref.shape[2])

        @pl.loop(begin, end)
        def _(r):
            cross_ref[r] = contract(trailing_ref[r], panel, 1, 1)

    ready = Gram.STAGES
    gram.wave(0)
    gram.wave(1)
    work_ref[...] = jnp.zeros_like(work_ref)
    gram.wave(2)
    multiply(0, rows // 2)
    gram.wave(3)
    gram.wave(4)
    multiply(rows // 2, rows)
    gram.wave(5)
    gram.wave(6)
    gram.place_chunk(0, work_ref, False)
    wide.start(1, 3)

    def beside(k):
        for w in range(ready, ready + len(chunks) - 1):
            @pl.when(k == w - ready)
            def _(w=w):
                gram.wave(w)
                gram.place_chunk(w - ready + 1, work_ref, w > ready)
                if w == ready:
                    wide.start(3, rows // 2 + 1)
        for s in range(1, rows // 2):
            pl.when(k == s + LATE)(lambda s=s: wide.fold(s))

    factor_loop(upper_ref, inverse_ref, work_ref, beside)
    upper_out[...] = upper_ref[
        pl.ds(pl.multiple_of(row * upper_out.shape[0], MICRO), upper_out.shape[0]),
        pl.ds(pl.multiple_of(col * upper_out.shape[1], BLOCK), upper_out.shape[1]),
    ]
    summed_ref[...] = wide.finish()
    solve(summed_ref, inverse_ref, middle_ref, slab_ref)
    spread_slab(rows, slab_ref, coef_out, *spreads)
    wide.drain()
    gram.drain()


def direct(panels_t, trailing_t, rows, cols):
    width, depth = panels_t.shape
    total = width * cols
    half = rows // 2
    trailing = trailing_t.reshape(rows, -1, depth)
    thick = trailing.shape[1]
    thin = width // (rows * cols)
    vmem = pl.BlockSpec(memory_space=pltpu.VMEM)
    shapes = [
        (cols, width, depth),
        (rows, thick, total),
        (half, thick, total),
        (half, thick, total),
        (total, total),
        (total, total),
        (total, total),
        (thick, total),
        (thick, total),
        (rows, thick, total // rows),
    ]
    chunks = gram_chunks(cols)
    staged = []
    for _, begin, end in chunks:
        wide = (end - begin) * width
        staged += [(2, half, thin, wide), (half, thin, wide), (half, thin, wide), (cols, 2, half, thin, wide)]
    semaphores = [pltpu.SemaphoreType.DMA((rows,))] * 2 + [pltpu.SemaphoreType.DMA((half,))] * 4
    steps = [1, half, half, 1, cols // 2, cols // 2]
    stepped = [pltpu.SemaphoreType.DMA((len(chunks), n)) for n in steps for _ in range(2)]
    r_block, spread = pl.pallas_call(
        lambda *refs: main_kernel(rows, cols, width, *refs),
        out_shape=(
            jax.ShapeDtypeStruct((total // rows, total // cols), jnp.float32),
            jax.ShapeDtypeStruct((rows, thick, total // rows), jnp.float32),
        ),
        in_specs=[vmem] * 2,
        out_specs=(vmem, vmem),
        scratch_shapes=[pltpu.VMEM(shape, jnp.float32) for shape in shapes]
        + semaphores
        + column_sems(cols, 2)
        + stepped
        + [pltpu.VMEM(shape, jnp.float32) for shape in staged],
        compiler_params=pltpu.CompilerParams(collective_id=1, has_side_effects=True, vmem_limit_bytes=48 * 1024 * 1024),
    )(panels_t, trailing)
    return r_block, spread.transpose(2, 0, 1).reshape(total // rows, -1)


def plain(panels_t, trailing_t):
    panel = lax.all_gather(panels_t, "col", axis=0, tiled=True)
    gram_part = lax.psum_scatter(product(panels_t, panel.T), "row", scatter_dimension=0, tiled=True)
    gram = lax.all_gather(gram_part, ("col", "row"), axis=0, tiled=True)
    cross = lax.psum_scatter(product(trailing_t, panel.T), "row", scatter_dimension=0, tiled=True)
    r_full, invert = factor(gram)
    slab = product(product(cross, invert.T), invert)
    return r_full, lax.all_to_all(slab, "row", split_axis=1, concat_axis=0, tiled=True).T


def local(panels_t, trailing_t):
    rows, cols = lax.axis_size("row"), lax.axis_size("col")
    width = panels_t.shape[0]
    total = width * cols
    thick = trailing_t.shape[0] // rows
    tiled = width % BLOCK == 0 and total // rows % BLOCK == 0 and width // rows % (cols * MICRO) == 0 and thick % MICRO == 0
    if tiled and rows % 2 == 0 and cols % 2 == 0 and rows // 2 + LATE < total // BLOCK and cols >= 4 and rows >= 4:
        return direct(panels_t, trailing_t, rows, cols)
    r_full, coef_block = plain(panels_t, trailing_t)
    rows_out = total // rows
    row_start = lax.axis_index("row") * rows_out
    col_start = lax.axis_index("col") * width
    r_block = lax.dynamic_slice(r_full, (row_start, col_start), (rows_out, width))
    return (r_block, coef_block)


def solution(mesh):
    placed = (P("col", "row"), P("col", "row"))
    return jax.shard_map(
        local,
        mesh=mesh,
        in_specs=placed,
        out_specs=(P("row", "col"), P("row", "col")),
        check_vma=False,
    )
```

```python
import jax
import jax.numpy as jnp
from jax import lax
from jax.experimental import pallas as pl
from jax.experimental.pallas import tpu as pltpu
from jax.sharding import PartitionSpec as P

BLOCK = 128
MICRO = 8
LATE = 1
MESH = pl.DeviceIdType.MESH


def product(left, right):
    return jnp.dot(left, right, precision=lax.Precision.HIGHEST)


def contract(left, right, left_dim, right_dim):
    return lax.dot_general(
        left,
        right,
        (((left_dim,), (right_dim,)), ((), ())),
        precision=lax.Precision.HIGHEST,
        preferred_element_type=jnp.float32,
    )


def lanes(tile, lane):
    return jnp.broadcast_to(tile[:, lane : lane + 1], tile.shape)


def sublanes(tile, row):
    return jnp.broadcast_to(tile[row : row + 1, :], tile.shape)


def factor_block(square):
    count = BLOCK // MICRO
    shape = (MICRO, BLOCK)
    row_id = lax.broadcasted_iota(jnp.int32, shape, 0)
    lane_id = lax.broadcasted_iota(jnp.int32, shape, 1)
    rest = [square[MICRO * i : MICRO * (i + 1), :] for i in range(count)]
    unit = [jnp.where(row_id + MICRO * i == lane_id, 1.0, 0.0) for i in range(count)]
    cols = [lanes(rest[0], c) for c in range(MICRO)]
    upper, inverse = [], []
    for b in range(count):
        base = MICRO * b
        tile, side = rest[b], unit[b]
        scales, pivots, rows, sides = [], {}, [], []
        upper_tile, side_tile = jnp.zeros(shape, jnp.float32), jnp.zeros(shape, jnp.float32)
        for k in range(MICRO):
            scale = lax.rsqrt(sublanes(cols[k], k))
            below = cols[k] * scale
            row = sublanes(tile, k) * scale
            side_row = sublanes(side, k) * scale
            for c in range(k + 1, MICRO):
                pivots[c, k] = sublanes(below, c)
                cols[c] = cols[c] - below * pivots[c, k]
            tile = tile - below * row
            side = side - below * side_row
            upper_tile = jnp.where(row_id == k, row, upper_tile)
            side_tile = jnp.where(row_id == k, side_row, side_tile)
            scales.append(scale)
            rows.append(row)
            sides.append(side_row)
        upper.append(jnp.where(row_id + base <= lane_id, upper_tile, 0.0))
        inverse.append(jnp.where(row_id + base >= lane_id, side_tile, 0.0))
        following = []
        for i in range(b + 1, count):
            tile, side = rest[i], unit[i]
            cols = [lanes(tile, base + c) for c in range(MICRO)]
            ahead = [lanes(tile, base + MICRO + c) for c in range(MICRO)] if i == b + 1 else []
            for k in range(MICRO):
                below = cols[k] * scales[k]
                for c in range(k + 1, MICRO):
                    cols[c] = cols[c] - below * pivots[c, k]
                for c in range(len(ahead)):
                    ahead[c] = ahead[c] - below * sublanes(below, c)
                tile = tile - below * rows[k]
                side = side - below * sides[k]
            rest[i], unit[i] = tile, side
            following = ahead or following
        cols = following
    return jnp.concatenate(upper, axis=0), jnp.concatenate(inverse, axis=0)


def factor_loop(upper_ref, inverse_ref, work_ref, beside):
    total = work_ref.shape[0]
    column = lax.broadcasted_iota(jnp.int32, (BLOCK, total), 1)

    @pl.loop(0, total // BLOCK)
    def _(k):
        start = pl.multiple_of(k * BLOCK, BLOCK)
        here = pl.ds(start, BLOCK)
        diagonal, inverse = factor_block(work_ref[here, here])
        beside(k)
        panel = product(inverse, work_ref[here, :])
        work_ref[here, :] = panel
        work_ref[here, here] = inverse
        upper_ref[here, :] = jnp.where(column >= start + BLOCK, panel, 0.0)
        upper_ref[here, here] = diagonal
        inverse_ref[here, :] = jnp.where(column < start, panel, 0.0)
        inverse_ref[here, here] = inverse

        @pl.loop(k + 1, total // BLOCK)
        def _(i):
            there = pl.ds(pl.multiple_of(i * BLOCK, BLOCK), BLOCK)
            work_ref[there, here] = jnp.zeros((BLOCK, BLOCK), jnp.float32)
            work_ref[there, :] -= contract(work_ref[here, there], work_ref[here, :], 0, 0)


def factor_kernel(gram_ref, upper_ref, inverse_ref, work_ref):
    work_ref[...] = gram_ref[...]
    factor_loop(upper_ref, inverse_ref, work_ref, lambda k: None)


def factor(gram):
    total = gram.shape[0]
    whole = jax.ShapeDtypeStruct((total, total), jnp.float32)
    return pl.pallas_call(
        factor_kernel,
        out_shape=(whole, whole),
        in_specs=[pl.BlockSpec(memory_space=pltpu.VMEM)],
        out_specs=(pl.BlockSpec(memory_space=pltpu.VMEM),) * 2,
        scratch_shapes=[pltpu.VMEM((total, total), jnp.float32)],
        compiler_params=pltpu.CompilerParams(vmem_limit_bytes=32 * 1024 * 1024),
        cost_estimate=pl.CostEstimate(flops=60 * total**3, bytes_accessed=12 * total**2, transcendentals=0),
    )(gram)


def remote(source, target, send, receive, row, col):
    return pltpu.make_async_remote_copy(
        src_ref=source,
        dst_ref=target,
        send_sem=send,
        recv_sem=receive,
        device_id=(row, col),
        device_id_type=MESH,
    )


def greet(peers):
    barrier = pltpu.get_barrier_semaphore()
    for row, col in peers:
        pl.semaphore_signal(barrier, inc=1, device_id=(row, col), device_id_type=MESH)
    pl.semaphore_wait(barrier, len(peers))


def column_peers(cols):
    row, col = lax.axis_index("row"), lax.axis_index("col")
    mate = col + 1 - 2 * lax.rem(col, 2)
    return [(row, lax.rem(col + 2 * t, cols)) for t in range(1, cols // 2)] + [(row, mate)]


def gather_columns(cols, pieces, ready, view, sems):
    line_send, line_recv, mate_send, mate_recv = sems
    row, col = lax.axis_index("row"), lax.axis_index("col")
    mate = col + 1 - 2 * lax.rem(col, 2)
    half = cols // 2
    sent = []

    def launch(copy):
        copy.start()
        sent.append(copy)

    def to_mate(source, owner, s, t):
        launch(remote(source, view(owner, s), mate_send.at[s, t], mate_recv.at[s, t], row, mate))

    def relay(s):
        for t in range(1, half):
            owner = lax.rem(col - 2 * t + cols, cols)
            place = view(owner, s)
            remote(place, place, line_send.at[s, t], line_recv.at[s, t], row, mate).wait_recv()
            to_mate(place, owner, s, t)

    for s in range(pieces):
        source = ready(s)
        for t in range(1, half):
            peer = lax.rem(col + 2 * t, cols)
            launch(remote(source, view(col, s), line_send.at[s, t], line_recv.at[s, t], row, peer))
        to_mate(source, col, s, 0)
        if s > 0:
            relay(s - 1)
    relay(pieces - 1)
    for s in range(pieces):
        for t in range(half):
            place = view(lax.rem(mate - 2 * t + cols, cols), s)
            remote(place, place, mate_send.at[s, t], mate_recv.at[s, t], row, mate).wait_recv()
    for copy in sent:
        copy.wait_send()


def column_sems(cols, pieces):
    return [pltpu.SemaphoreType.DMA((pieces, cols // 2))] * 4


def gather_panel(cols, block_ref, panel_ref, sems):
    pieces = sems[0].shape[0]
    size = block_ref.shape[0] // pieces

    def part(s):
        return pl.ds(s * size, size)

    gather_columns(cols, pieces, lambda s: block_ref.at[part(s)], lambda c, s: panel_ref.at[c, part(s)], sems)
    panel_ref[lax.axis_index("col")] = block_ref[...]


class Reduction:
    def __init__(self, rows, buffer_ref, pair_ref, line_ref, pairs, lines):
        self.buffer, self.pair, self.line = buffer_ref, pair_ref, line_ref
        self.pairs, self.lines = pairs, lines
        self.row, self.col = lax.axis_index("row"), lax.axis_index("col")
        self.half = rows // 2
        self.place, self.side = self.row // 2, lax.rem(self.row, 2)

    def target(self, s, which):
        return 2 * lax.rem(self.place + s, self.half) + which

    def pair_copy(self, s):
        mate = 2 * self.place + 1 - self.side
        source = self.buffer.at[self.target(s, 1 - self.side)]
        return remote(source, self.pair.at[s], self.pairs[0].at[s], self.pairs[1].at[s], mate, self.col)

    def line_copy(self, s):
        owner = self.target(s, self.side)
        source = self.buffer.at[owner]
        return remote(source, self.line.at[s], self.lines[0].at[s], self.lines[1].at[s], owner, self.col)

    def start(self, begin, end):
        for s in range(begin, end):
            self.pair_copy(s % self.half).start()

    def fold(self, s):
        self.pair_copy(s).wait_recv()
        self.buffer[self.target(s, self.side)] += self.pair[s]
        if s > 0:
            self.line_copy(s).start()

    def finish(self):
        self.fold(0)
        total = self.buffer[self.row]
        for s in range(1, self.half):
            self.line_copy(s).wait_recv()
            total = total + self.line[s]
        return total

    def drain(self):
        for s in range(self.half):
            self.pair_copy(s).wait_send()
            if s > 0:
                self.line_copy(s).wait_send()


class Gram:
    STAGES = 7

    def __init__(self, rows, cols, width, panel_ref, buffers, sems):
        self.rows, self.cols, self.width, self.panel = rows, cols, width, panel_ref
        self.buffers, self.sems = buffers, sems
        self.row, self.col = lax.axis_index("row"), lax.axis_index("col")
        self.half, self.across = rows // 2, cols // 2
        self.place, self.side = self.row // 2, lax.rem(self.row, 2)
        self.beside = 2 * self.place + 1 - self.side
        self.mate = self.col + 1 - 2 * lax.rem(self.col, 2)
        self.chunks = gram_chunks(cols, width // BLOCK)

    def put(self, source, target, which, ch, n, row, col):
        send, receive = self.sems[which]
        copy = remote(source, target, send.at[ch, n], receive.at[ch, n], row, col)
        copy.start()

    def got(self, place, which, ch, n):
        send, receive = self.sems[which]
        remote(place, place, send.at[ch, n], receive.at[ch, n], self.beside, self.col).wait_recv()

    def peer(self, s):
        return lax.rem(self.place + s, self.half)

    def stage(self, ch, st):
        own, first, last = self.chunks[ch]
        part, pair, line, full = self.buffers[ch]
        side, col = self.side, self.col
        thin = part.shape[2]
        if st == 0:
            if first is None:
                strip = self.panel[0, own * BLOCK : (own + 1) * BLOCK, :]
                right = self.panel[col]
            else:
                strip = self.panel[own, pl.ds(pl.multiple_of(col * (thin * self.rows), MICRO), thin * self.rows), :]
                right = self.panel[first:last].reshape((last - first) * self.width, -1)
            held = contract(strip, right, 1, 1)
            for r in range(self.rows):
                part[r % 2, r // 2] = held[r * thin : (r + 1) * thin]
            self.put(part.at[1 - side], pair, 0, ch, 0, self.beside, col)
        if st == 1:
            self.got(pair, 0, ch, 0)
            for s in range(self.half):
                part[side, s] += pair[s]
            for s in range(1, self.half):
                to = self.peer(s)
                self.put(part.at[side, to], line.at[s], 1, ch, s, 2 * to + side, col)
        if st == 2:
            total = part[side, self.place]
            for s in range(1, self.half):
                self.got(line.at[s], 1, ch, s)
                total = total + line[s]
            mine = full.at[col, side, self.place]
            full[col, side, self.place] = total
            for s in range(1, self.half):
                self.put(mine, mine, 2, ch, s, 2 * self.peer(s) + side, col)
        if st == 3:
            for s in range(1, self.half):
                self.got(full.at[col, side, self.peer(self.half - s)], 2, ch, s)
            mine = full.at[col, side]
            self.put(mine, mine, 3, ch, 0, self.beside, col)
        if st == 4:
            self.got(full.at[col, 1 - side], 3, ch, 0)
            mine = full.at[col]
            for t in range(1, self.across):
                self.put(mine, mine, 4, ch, t, self.row, lax.rem(col + 2 * t, self.cols))
            self.put(mine, mine, 5, ch, 0, self.row, self.mate)
        if st == 5:
            for t in range(1, self.across):
                place = full.at[lax.rem(col - 2 * t + self.cols, self.cols)]
                self.got(place, 4, ch, t)
                self.put(place, place, 5, ch, t, self.row, self.mate)
        if st == 6:
            for t in range(self.across):
                self.got(full.at[lax.rem(self.mate - 2 * t + self.cols, self.cols)], 5, ch, t)

    def wave(self, w):
        for ch in range(len(self.chunks)):
            if 0 <= w - ch < self.STAGES:
                self.stage(ch, w - ch)

    def place_chunk(self, ch, work_ref, add):
        own, first, last = self.chunks[ch]
        full = self.buffers[ch][3]
        thin = full.shape[3]
        for c in range(self.cols):
            for r in range(self.rows):
                if first is None:
                    there = pl.ds(own * BLOCK + r * thin, thin)
                    columns = pl.ds(c * self.width, self.width)
                else:
                    there = pl.ds(own * self.width + (c * self.rows + r) * thin, thin)
                    columns = pl.ds(first * self.width, (last - first) * self.width)
                held = full[c, r % 2, r // 2]
                work_ref[there, columns] = work_ref[there, columns] + held if add else held

    def drain(self):
        for ch, (part, pair, line, full) in enumerate(self.buffers):
            one, all_places, strip = full.at[0, 0, 0], full.at[0, 0], full.at[0]
            steps = [(0, 0, pair)] + [(1, s, one) for s in range(1, self.half)] + [(2, s, one) for s in range(1, self.half)]
            steps += [(3, 0, all_places)] + [(4, t, strip) for t in range(1, self.across)]
            steps += [(5, t, strip) for t in range(self.across)]
            for which, n, place in steps:
                send, receive = self.sems[which]
                remote(place, place, send.at[ch, n], receive.at[ch, n], self.beside, self.col).wait_send()


def gram_chunks(cols, halves):
    return [(h, None, None) for h in range(halves)] + [(q, q, cols) for q in range(1, cols)]


def chunk_shape(chunk, rows, cols, width):
    _, begin, end = chunk
    if begin is None:
        return BLOCK // rows, width
    return width // (rows * cols), (end - begin) * width


def solve(rows, cross_ref, inverse_ref, middle_ref, slab_ref, out_ref, send, receive):
    row, col = lax.axis_index("row"), lax.axis_index("col")
    total = inverse_ref.shape[0]
    step = 2 * BLOCK
    for j in range(0, total, step):
        stop = j + step
        middle_ref[:, j:stop] = contract(cross_ref[:, :stop], inverse_ref[j:stop, :stop], 1, 1)
    wide = total // slab_ref.shape[0]
    for j in range(0, total, step):
        found = contract(middle_ref[:, j:], inverse_ref[j:, j : j + step], 1, 0)
        for t in range(0, step, wide):
            peer = (j + t) // wide
            slab_ref[peer] = found[:, t : t + wide]

            @pl.when(row != peer)
            def _(peer=peer):
                s = lax.rem(peer - row + rows, rows)
                remote(slab_ref.at[peer], out_ref.at[row], send.at[s], receive.at[s], peer, col).start()


def settle_slab(rows, slab_ref, out_ref, send, receive):
    row, col = lax.axis_index("row"), lax.axis_index("col")
    out_ref[row] = slab_ref[row]
    for s in range(1, rows):
        place = out_ref.at[lax.rem(row - s + rows, rows)]
        remote(place, place, send.at[s], receive.at[s], lax.rem(row + s, rows), col).wait_recv()
    for s in range(1, rows):
        place = slab_ref.at[lax.rem(row + s, rows)]
        remote(place, place, send.at[s], receive.at[s], lax.rem(row + s, rows), col).wait_send()


def main_kernel(rows, cols, width, *refs):
    block_ref, trailing_ref, upper_out, coef_out, panel_ref = refs[:5]
    cross_ref, pair_ref, line_ref, work_ref, upper_ref, inverse_ref, summed_ref, middle_ref, slab_ref = refs[5:14]
    spreads, pairs, lines = (refs[14 + 2 * i : 16 + 2 * i] for i in range(3))
    first = refs[20:24]
    steps = [refs[24 + 2 * i : 26 + 2 * i] for i in range(6)]
    chunks = gram_chunks(cols, width // BLOCK)
    buffers = [refs[36 + 4 * i : 40 + 4 * i] for i in range(len(chunks))]
    row, col = lax.axis_index("row"), lax.axis_index("col")
    greet([(lax.rem(row + s, rows), col) for s in range(1, rows)] + column_peers(cols))
    gather_panel(cols, block_ref, panel_ref, first)
    gram = Gram(rows, cols, width, panel_ref, buffers, steps)
    wide = Reduction(rows, cross_ref, pair_ref, line_ref, pairs, lines)
    total = work_ref.shape[0]

    def multiply(begin, end):
        panel = panel_ref[...].reshape(width * cols, panel_ref.shape[2])

        @pl.loop(begin, end)
        def _(r):
            cross_ref[r] = contract(trailing_ref[r], panel, 1, 1)

    ready = Gram.STAGES
    gram.wave(0)
    work_ref[...] = jnp.zeros_like(work_ref)
    gram.wave(1)
    multiply(0, rows // 4)
    gram.wave(2)
    multiply(rows // 4, rows // 2)
    gram.wave(3)
    multiply(rows // 2, 3 * rows // 4)
    gram.wave(4)
    multiply(3 * rows // 4, rows)
    gram.wave(5)
    gram.wave(6)
    gram.place_chunk(0, work_ref, False)

    def beside(k):
        for w in range(ready, ready + len(chunks) - 1):
            @pl.when(k == w - ready)
            def _(w=w):
                gram.wave(w)
                gram.place_chunk(w - ready + 1, work_ref, w > ready)
                if w == ready:
                    wide.start(1, rows // 2 + 1)
        for s in range(1, rows // 2):
            pl.when(k == s + LATE)(lambda s=s: wide.fold(s))

    factor_loop(upper_ref, inverse_ref, work_ref, beside)
    upper_out[...] = upper_ref[
        pl.ds(pl.multiple_of(row * upper_out.shape[0], MICRO), upper_out.shape[0]),
        pl.ds(pl.multiple_of(col * upper_out.shape[1], BLOCK), upper_out.shape[1]),
    ]
    summed_ref[...] = wide.finish()
    solve(rows, summed_ref, inverse_ref, middle_ref, slab_ref, coef_out, *spreads)
    settle_slab(rows, slab_ref, coef_out, *spreads)
    wide.drain()
    gram.drain()


def direct(panels_t, trailing_t, rows, cols):
    width, depth = panels_t.shape
    total = width * cols
    half = rows // 2
    trailing = trailing_t.reshape(rows, -1, depth)
    thick = trailing.shape[1]
    vmem = pl.BlockSpec(memory_space=pltpu.VMEM)
    shapes = [
        (cols, width, depth),
        (rows, thick, total),
        (half, thick, total),
        (half, thick, total),
        (total, total),
        (total, total),
        (total, total),
        (thick, total),
        (thick, total),
        (rows, thick, total // rows),
    ]
    chunks = gram_chunks(cols, width // BLOCK)
    staged = []
    for chunk in chunks:
        thin, wide = chunk_shape(chunk, rows, cols, width)
        staged += [(2, half, thin, wide), (half, thin, wide), (half, thin, wide), (cols, 2, half, thin, wide)]
    semaphores = [pltpu.SemaphoreType.DMA((rows,))] * 2 + [pltpu.SemaphoreType.DMA((half,))] * 4
    steps = [1, half, half, 1, cols // 2, cols // 2]
    stepped = [pltpu.SemaphoreType.DMA((len(chunks), n)) for n in steps for _ in range(2)]
    r_block, spread = pl.pallas_call(
        lambda *refs: main_kernel(rows, cols, width, *refs),
        out_shape=(
            jax.ShapeDtypeStruct((total // rows, total // cols), jnp.float32),
            jax.ShapeDtypeStruct((rows, thick, total // rows), jnp.float32),
        ),
        in_specs=[vmem] * 2,
        out_specs=(vmem, vmem),
        scratch_shapes=[pltpu.VMEM(shape, jnp.float32) for shape in shapes]
        + semaphores
        + column_sems(cols, 2)
        + stepped
        + [pltpu.VMEM(shape, jnp.float32) for shape in staged],
        compiler_params=pltpu.CompilerParams(collective_id=1, has_side_effects=True, vmem_limit_bytes=48 * 1024 * 1024),
    )(panels_t, trailing)
    return r_block, spread.transpose(2, 0, 1).reshape(total // rows, -1)


def plain(panels_t, trailing_t):
    panel = lax.all_gather(panels_t, "col", axis=0, tiled=True)
    gram_part = lax.psum_scatter(product(panels_t, panel.T), "row", scatter_dimension=0, tiled=True)
    gram = lax.all_gather(gram_part, ("col", "row"), axis=0, tiled=True)
    cross = lax.psum_scatter(product(trailing_t, panel.T), "row", scatter_dimension=0, tiled=True)
    r_full, invert = factor(gram)
    slab = product(product(cross, invert.T), invert)
    return r_full, lax.all_to_all(slab, "row", split_axis=1, concat_axis=0, tiled=True).T


def local(panels_t, trailing_t):
    rows, cols = lax.axis_size("row"), lax.axis_size("col")
    width = panels_t.shape[0]
    total = width * cols
    thick = trailing_t.shape[0] // rows
    tiled = width % BLOCK == 0 and total // rows % BLOCK == 0 and width // rows % (cols * MICRO) == 0 and thick % MICRO == 0
    if tiled and rows % 2 == 0 and cols % 2 == 0 and rows // 2 + LATE < total // BLOCK and cols >= 4 and rows % 4 == 0 and BLOCK % (rows * MICRO) == 0 and width == 2 * BLOCK:
        return direct(panels_t, trailing_t, rows, cols)
    r_full, coef_block = plain(panels_t, trailing_t)
    rows_out = total // rows
    row_start = lax.axis_index("row") * rows_out
    col_start = lax.axis_index("col") * width
    r_block = lax.dynamic_slice(r_full, (row_start, col_start), (rows_out, width))
    return (r_block, coef_block)


def solution(mesh):
    placed = (P("col", "row"), P("col", "row"))
    return jax.shard_map(
        local,
        mesh=mesh,
        in_specs=placed,
        out_specs=(P("row", "col"), P("row", "col")),
        check_vma=False,
    )
```

```python
import jax
import jax.numpy as jnp
from jax import lax
from jax.experimental import pallas as pl
from jax.experimental.pallas import tpu as pltpu
from jax.sharding import PartitionSpec as P

BLOCK = 128
MICRO = 8
LATE = 0
MESH = pl.DeviceIdType.MESH


def product(left, right):
    return jnp.dot(left, right, precision=lax.Precision.HIGHEST)


def contract(left, right, left_dim, right_dim):
    return lax.dot_general(
        left,
        right,
        (((left_dim,), (right_dim,)), ((), ())),
        precision=lax.Precision.HIGHEST,
        preferred_element_type=jnp.float32,
    )


def lanes(tile, lane):
    return jnp.broadcast_to(tile[:, lane : lane + 1], tile.shape)


def sublanes(tile, row):
    return jnp.broadcast_to(tile[row : row + 1, :], tile.shape)


def factor_block(square):
    count = BLOCK // MICRO
    shape = (MICRO, BLOCK)
    row_id = lax.broadcasted_iota(jnp.int32, shape, 0)
    lane_id = lax.broadcasted_iota(jnp.int32, shape, 1)
    rest = [square[MICRO * i : MICRO * (i + 1), :] for i in range(count)]
    unit = [jnp.where(row_id + MICRO * i == lane_id, 1.0, 0.0) for i in range(count)]
    cols = [lanes(rest[0], c) for c in range(MICRO)]
    upper, inverse = [], []
    for b in range(count):
        base = MICRO * b
        tile, side = rest[b], unit[b]
        scales, pivots, rows, sides = [], {}, [], []
        upper_tile, side_tile = jnp.zeros(shape, jnp.float32), jnp.zeros(shape, jnp.float32)
        for k in range(MICRO):
            scale = lax.rsqrt(sublanes(cols[k], k))
            below = cols[k] * scale
            row = sublanes(tile, k) * scale
            side_row = sublanes(side, k) * scale
            for c in range(k + 1, MICRO):
                pivots[c, k] = sublanes(below, c)
                cols[c] = cols[c] - below * pivots[c, k]
            tile = tile - below * row
            side = side - below * side_row
            upper_tile = jnp.where(row_id == k, row, upper_tile)
            side_tile = jnp.where(row_id == k, side_row, side_tile)
            scales.append(scale)
            rows.append(row)
            sides.append(side_row)
        upper.append(jnp.where(row_id + base <= lane_id, upper_tile, 0.0))
        inverse.append(jnp.where(row_id + base >= lane_id, side_tile, 0.0))
        following = []
        for i in range(b + 1, count):
            tile, side = rest[i], unit[i]
            cols = [lanes(tile, base + c) for c in range(MICRO)]
            ahead = [lanes(tile, base + MICRO + c) for c in range(MICRO)] if i == b + 1 else []
            for k in range(MICRO):
                below = cols[k] * scales[k]
                for c in range(k + 1, MICRO):
                    cols[c] = cols[c] - below * pivots[c, k]
                for c in range(len(ahead)):
                    ahead[c] = ahead[c] - below * sublanes(below, c)
                tile = tile - below * rows[k]
                side = side - below * sides[k]
            rest[i], unit[i] = tile, side
            following = ahead or following
        cols = following
    return jnp.concatenate(upper, axis=0), jnp.concatenate(inverse, axis=0)


def factor_loop(upper_ref, inverse_ref, work_ref, beside):
    total = work_ref.shape[0]
    column = lax.broadcasted_iota(jnp.int32, (BLOCK, total), 1)

    @pl.loop(0, total // BLOCK)
    def _(k):
        start = pl.multiple_of(k * BLOCK, BLOCK)
        here = pl.ds(start, BLOCK)
        diagonal, inverse = factor_block(work_ref[here, here])
        beside(k)
        panel = product(inverse, work_ref[here, :])
        work_ref[here, :] = panel
        work_ref[here, here] = inverse
        upper_ref[here, :] = jnp.where(column >= start + BLOCK, panel, 0.0)
        upper_ref[here, here] = diagonal
        inverse_ref[here, :] = jnp.where(column < start, panel, 0.0)
        inverse_ref[here, here] = inverse

        def update(begin, size):
            there = pl.ds(pl.multiple_of(begin * BLOCK, BLOCK), size)
            work_ref[there, here] = jnp.zeros((size, BLOCK), jnp.float32)
            work_ref[there, :] -= contract(work_ref[here, there], work_ref[here, :], 0, 0)

        left = total // BLOCK - 1 - k
        odd = lax.rem(left, 2)
        pl.when(odd == 1)(lambda: update(k + 1, BLOCK))

        @pl.loop(0, left // 2)
        def _(i):
            update(k + 1 + odd + 2 * i, 2 * BLOCK)


def factor_kernel(gram_ref, upper_ref, inverse_ref, work_ref):
    work_ref[...] = gram_ref[...]
    factor_loop(upper_ref, inverse_ref, work_ref, lambda k: None)


def factor(gram):
    total = gram.shape[0]
    whole = jax.ShapeDtypeStruct((total, total), jnp.float32)
    return pl.pallas_call(
        factor_kernel,
        out_shape=(whole, whole),
        in_specs=[pl.BlockSpec(memory_space=pltpu.VMEM)],
        out_specs=(pl.BlockSpec(memory_space=pltpu.VMEM),) * 2,
        scratch_shapes=[pltpu.VMEM((total, total), jnp.float32)],
        compiler_params=pltpu.CompilerParams(vmem_limit_bytes=32 * 1024 * 1024),
        cost_estimate=pl.CostEstimate(flops=60 * total**3, bytes_accessed=12 * total**2, transcendentals=0),
    )(gram)


def remote(source, target, send, receive, row, col):
    return pltpu.make_async_remote_copy(
        src_ref=source,
        dst_ref=target,
        send_sem=send,
        recv_sem=receive,
        device_id=(row, col),
        device_id_type=MESH,
    )


def greet(peers):
    barrier = pltpu.get_barrier_semaphore()
    for row, col in peers:
        pl.semaphore_signal(barrier, inc=1, device_id=(row, col), device_id_type=MESH)
    pl.semaphore_wait(barrier, len(peers))


def column_peers(cols):
    row, col = lax.axis_index("row"), lax.axis_index("col")
    mate = col + 1 - 2 * lax.rem(col, 2)
    return [(row, lax.rem(col + 2 * t, cols)) for t in range(1, cols // 2)] + [(row, mate)]


def gather_columns(cols, pieces, ready, view, sems, early):
    line_send, line_recv, mate_send, mate_recv = sems
    row, col = lax.axis_index("row"), lax.axis_index("col")
    mate = col + 1 - 2 * lax.rem(col, 2)
    half = cols // 2
    sent = []

    def launch(copy):
        copy.start()
        sent.append(copy)

    def to_mate(source, owner, s, t):
        launch(remote(source, view(owner, s), mate_send.at[s, t], mate_recv.at[s, t], row, mate))

    def relay(s):
        for t in range(1, half):
            owner = lax.rem(col - 2 * t + cols, cols)
            place = view(owner, s)
            remote(place, place, line_send.at[s, t], line_recv.at[s, t], row, mate).wait_recv()
            to_mate(place, owner, s, t)

    for s in range(pieces):
        source = ready(s)
        for t in range(1, half):
            peer = lax.rem(col + 2 * t, cols)
            launch(remote(source, view(col, s), line_send.at[s, t], line_recv.at[s, t], row, peer))
        to_mate(source, col, s, 0)
        if s > 0:
            relay(s - 1)
    for s in range(pieces):
        if s == pieces - 1:
            relay(s)
        for t in range(half):
            place = view(lax.rem(mate - 2 * t + cols, cols), s)
            remote(place, place, mate_send.at[s, t], mate_recv.at[s, t], row, mate).wait_recv()
        if s == 0:
            early()
    for copy in sent:
        copy.wait_send()


def column_sems(cols, pieces):
    return [pltpu.SemaphoreType.DMA((pieces, cols // 2))] * 4


def gather_panel(cols, block_ref, panel_ref, sems, early):
    pieces = sems[0].shape[0]
    size = block_ref.shape[0] // pieces

    def part(s):
        return pl.ds(s * size, size)

    panel_ref[lax.axis_index("col")] = block_ref[...]
    gather_columns(cols, pieces, lambda s: block_ref.at[part(s)], lambda c, s: panel_ref.at[c, part(s)], sems, early)


class Reduction:
    def __init__(self, rows, buffer_ref, pair_ref, line_ref, pairs, lines):
        self.buffer, self.pair, self.line = buffer_ref, pair_ref, line_ref
        self.pairs, self.lines = pairs, lines
        self.row, self.col = lax.axis_index("row"), lax.axis_index("col")
        self.half = rows // 2
        self.place, self.side = self.row // 2, lax.rem(self.row, 2)

    def target(self, s, which):
        return 2 * lax.rem(self.place + s, self.half) + which

    def pair_copy(self, s):
        mate = 2 * self.place + 1 - self.side
        source = self.buffer.at[self.target(s, 1 - self.side)]
        return remote(source, self.pair.at[s], self.pairs[0].at[s], self.pairs[1].at[s], mate, self.col)

    def line_copy(self, s):
        owner = self.target(s, self.side)
        source = self.buffer.at[owner]
        return remote(source, self.line.at[s], self.lines[0].at[s], self.lines[1].at[s], owner, self.col)

    def start(self, begin, end):
        for s in range(begin, end):
            self.pair_copy(s % self.half).start()

    def fold(self, s):
        self.pair_copy(s).wait_recv()
        self.buffer[self.target(s, self.side)] += self.pair[s]
        if s > 0:
            self.line_copy(s).start()

    def finish(self):
        self.fold(0)
        total = self.buffer[self.row]
        for s in range(1, self.half):
            self.line_copy(s).wait_recv()
            total = total + self.line[s]
        return total

    def drain(self):
        for s in range(self.half):
            self.pair_copy(s).wait_send()
            if s > 0:
                self.line_copy(s).wait_send()


class Gram:
    STAGES = 7

    def __init__(self, rows, cols, width, block_ref, panel_ref, buffers, sems):
        self.block = block_ref
        self.rows, self.cols, self.width, self.panel = rows, cols, width, panel_ref
        self.buffers, self.sems = buffers, sems
        self.row, self.col = lax.axis_index("row"), lax.axis_index("col")
        self.half, self.across = rows // 2, cols // 2
        self.place, self.side = self.row // 2, lax.rem(self.row, 2)
        self.beside = 2 * self.place + 1 - self.side
        self.mate = self.col + 1 - 2 * lax.rem(self.col, 2)
        self.chunks = gram_chunks(cols, width // BLOCK)

    def put(self, source, target, which, ch, n, row, col):
        send, receive = self.sems[which]
        copy = remote(source, target, send.at[ch, n], receive.at[ch, n], row, col)
        copy.start()

    def got(self, place, which, ch, n):
        send, receive = self.sems[which]
        remote(place, place, send.at[ch, n], receive.at[ch, n], self.beside, self.col).wait_recv()

    def peer(self, s):
        return lax.rem(self.place + s, self.half)

    def stage(self, ch, st):
        own, first, last = self.chunks[ch]
        part, pair, line, full = self.buffers[ch]
        side, col = self.side, self.col
        thin = part.shape[2]
        if st == 0:
            if first is None:
                strip = self.panel[0, own * BLOCK : (own + 1) * BLOCK, :]
                right = self.block[...]
            else:
                strip = self.panel[own, pl.ds(pl.multiple_of(col * (thin * self.rows), MICRO), thin * self.rows), :]
                right = self.panel[first:last].reshape((last - first) * self.width, -1)
            held = contract(strip, right, 1, 1)
            for r in range(self.rows):
                part[r % 2, r // 2] = held[r * thin : (r + 1) * thin]
            self.put(part.at[1 - side], pair, 0, ch, 0, self.beside, col)
        if st == 1:
            self.got(pair, 0, ch, 0)
            for s in range(self.half):
                part[side, s] += pair[s]
            for s in range(1, self.half):
                to = self.peer(s)
                self.put(part.at[side, to], line.at[s], 1, ch, s, 2 * to + side, col)
        if st == 2:
            total = part[side, self.place]
            for s in range(1, self.half):
                self.got(line.at[s], 1, ch, s)
                total = total + line[s]
            mine = full.at[col, side, self.place]
            full[col, side, self.place] = total
            for s in range(1, self.half):
                self.put(mine, mine, 2, ch, s, 2 * self.peer(s) + side, col)
        if st == 3:
            for s in range(1, self.half):
                self.got(full.at[col, side, self.peer(self.half - s)], 2, ch, s)
            mine = full.at[col, side]
            self.put(mine, mine, 3, ch, 0, self.beside, col)
        if st == 4:
            self.got(full.at[col, 1 - side], 3, ch, 0)
            mine = full.at[col]
            for t in range(1, self.across):
                self.put(mine, mine, 4, ch, t, self.row, lax.rem(col + 2 * t, self.cols))
            self.put(mine, mine, 5, ch, 0, self.row, self.mate)
        if st == 5:
            for t in range(1, self.across):
                place = full.at[lax.rem(col - 2 * t + self.cols, self.cols)]
                self.got(place, 4, ch, t)
                self.put(place, place, 5, ch, t, self.row, self.mate)
        if st == 6:
            for t in range(self.across):
                self.got(full.at[lax.rem(self.mate - 2 * t + self.cols, self.cols)], 5, ch, t)

    def wave(self, w):
        for ch in range(len(self.chunks)):
            if 0 <= w - self.lag(ch) < self.STAGES:
                self.stage(ch, w - self.lag(ch))

    def lag(self, ch):
        return ch + (ch == len(self.chunks) - 1)

    def place_chunk(self, ch, work_ref, add):
        own, first, last = self.chunks[ch]
        full = self.buffers[ch][3]
        thin = full.shape[3]
        for c in range(self.cols):
            for r in range(self.rows):
                if first is None:
                    there = pl.ds(own * BLOCK + r * thin, thin)
                    columns = pl.ds(c * self.width, self.width)
                else:
                    there = pl.ds(own * self.width + (c * self.rows + r) * thin, thin)
                    columns = pl.ds(first * self.width, (last - first) * self.width)
                held = full[c, r % 2, r // 2]
                work_ref[there, columns] = work_ref[there, columns] + held if add else held

    def drain(self):
        for ch, (part, pair, line, full) in enumerate(self.buffers):
            one, all_places, strip = full.at[0, 0, 0], full.at[0, 0], full.at[0]
            steps = [(0, 0, pair)] + [(1, s, one) for s in range(1, self.half)] + [(2, s, one) for s in range(1, self.half)]
            steps += [(3, 0, all_places)] + [(4, t, strip) for t in range(1, self.across)]
            steps += [(5, t, strip) for t in range(self.across)]
            for which, n, place in steps:
                send, receive = self.sems[which]
                remote(place, place, send.at[ch, n], receive.at[ch, n], self.beside, self.col).wait_send()


def gram_chunks(cols, halves):
    return [(h, None, None) for h in range(halves)] + [(q, q, cols) for q in range(1, cols)]


def chunk_shape(chunk, rows, cols, width):
    _, begin, end = chunk
    if begin is None:
        return BLOCK // rows, width
    return width // (rows * cols), (end - begin) * width


def solve(rows, cross_ref, inverse_ref, middle_ref, slab_ref, out_ref, send, receive):
    row, col = lax.axis_index("row"), lax.axis_index("col")
    total = inverse_ref.shape[0]
    step = 2 * BLOCK
    for j in range(0, total, step):
        stop = j + step
        middle_ref[:, j:stop] = contract(cross_ref[:, :stop], inverse_ref[j:stop, :stop], 1, 1)
    wide = total // slab_ref.shape[0]
    for j in range(0, total, step):
        found = contract(middle_ref[:, j:], inverse_ref[j:, j : j + step], 1, 0)
        for t in range(0, step, wide):
            peer = (j + t) // wide
            slab_ref[peer] = found[:, t : t + wide]

            @pl.when(row != peer)
            def _(peer=peer):
                s = lax.rem(peer - row + rows, rows)
                remote(slab_ref.at[peer], out_ref.at[row], send.at[s], receive.at[s], peer, col).start()


def settle_slab(rows, slab_ref, out_ref, send, receive):
    row, col = lax.axis_index("row"), lax.axis_index("col")
    out_ref[row] = slab_ref[row]
    for s in range(1, rows):
        place = out_ref.at[lax.rem(row - s + rows, rows)]
        remote(place, place, send.at[s], receive.at[s], lax.rem(row + s, rows), col).wait_recv()
    for s in range(1, rows):
        place = slab_ref.at[lax.rem(row + s, rows)]
        remote(place, place, send.at[s], receive.at[s], lax.rem(row + s, rows), col).wait_send()


def main_kernel(rows, cols, width, *refs):
    block_ref, trailing_ref, upper_out, coef_out, panel_ref = refs[:5]
    cross_ref, pair_ref, line_ref, work_ref, upper_ref, inverse_ref, summed_ref, middle_ref, slab_ref = refs[5:14]
    spreads, pairs, lines = (refs[14 + 2 * i : 16 + 2 * i] for i in range(3))
    first = refs[20:24]
    steps = [refs[24 + 2 * i : 26 + 2 * i] for i in range(6)]
    chunks = gram_chunks(cols, width // BLOCK)
    buffers = [refs[36 + 4 * i : 40 + 4 * i] for i in range(len(chunks))]
    row, col = lax.axis_index("row"), lax.axis_index("col")
    greet([(lax.rem(row + s, rows), col) for s in range(1, rows)] + column_peers(cols))
    gram = Gram(rows, cols, width, block_ref, panel_ref, buffers, steps)
    gather_panel(cols, block_ref, panel_ref, first, lambda: gram.wave(0))
    wide = Reduction(rows, cross_ref, pair_ref, line_ref, pairs, lines)
    total = work_ref.shape[0]

    def multiply(begin, end):
        panel = panel_ref[...].reshape(width * cols, panel_ref.shape[2])

        @pl.loop(begin, end)
        def _(r):
            cross_ref[r] = contract(trailing_ref[r], panel, 1, 1)

    ready = Gram.STAGES
    work_ref[...] = jnp.zeros_like(work_ref)
    gram.wave(1)
    multiply(0, rows // 4)
    gram.wave(2)
    multiply(rows // 4, rows // 2)
    gram.wave(3)
    multiply(rows // 2, 3 * rows // 4)
    gram.wave(4)
    multiply(3 * rows // 4, rows)
    gram.wave(5)
    gram.wave(6)
    gram.place_chunk(0, work_ref, False)
    wide.start(1, 2)

    def beside(k):
        for w in range(ready, ready + len(chunks)):
            @pl.when(k == w - ready)
            def _(w=w):
                gram.wave(w)
                for ch in range(1, len(chunks)):
                    if gram.lag(ch) + ready - 1 == w:
                        gram.place_chunk(ch, work_ref, ch > 1)
                if w == ready:
                    wide.start(2, 3)
                if w == ready + 1:
                    wide.start(3, rows // 2 + 1)
        for s in range(1, rows // 2):
            pl.when(k == s + LATE)(lambda s=s: wide.fold(s))

    factor_loop(upper_ref, inverse_ref, work_ref, beside)
    upper_out[...] = upper_ref[
        pl.ds(pl.multiple_of(row * upper_out.shape[0], MICRO), upper_out.shape[0]),
        pl.ds(pl.multiple_of(col * upper_out.shape[1], BLOCK), upper_out.shape[1]),
    ]
    summed_ref[...] = wide.finish()
    solve(rows, summed_ref, inverse_ref, middle_ref, slab_ref, coef_out, *spreads)
    settle_slab(rows, slab_ref, coef_out, *spreads)
    wide.drain()
    gram.drain()


def direct(panels_t, trailing_t, rows, cols):
    width, depth = panels_t.shape
    total = width * cols
    half = rows // 2
    trailing = trailing_t.reshape(rows, -1, depth)
    thick = trailing.shape[1]
    vmem = pl.BlockSpec(memory_space=pltpu.VMEM)
    shapes = [
        (cols, width, depth),
        (rows, thick, total),
        (half, thick, total),
        (half, thick, total),
        (total, total),
        (total, total),
        (total, total),
        (thick, total),
        (thick, total),
        (rows, thick, total // rows),
    ]
    chunks = gram_chunks(cols, width // BLOCK)
    staged = []
    for chunk in chunks:
        thin, wide = chunk_shape(chunk, rows, cols, width)
        staged += [(2, half, thin, wide), (half, thin, wide), (half, thin, wide), (cols, 2, half, thin, wide)]
    semaphores = [pltpu.SemaphoreType.DMA((rows,))] * 2 + [pltpu.SemaphoreType.DMA((half,))] * 4
    steps = [1, half, half, 1, cols // 2, cols // 2]
    stepped = [pltpu.SemaphoreType.DMA((len(chunks), n)) for n in steps for _ in range(2)]
    r_block, spread = pl.pallas_call(
        lambda *refs: main_kernel(rows, cols, width, *refs),
        out_shape=(
            jax.ShapeDtypeStruct((total // rows, total // cols), jnp.float32),
            jax.ShapeDtypeStruct((rows, thick, total // rows), jnp.float32),
        ),
        in_specs=[vmem] * 2,
        out_specs=(vmem, vmem),
        scratch_shapes=[pltpu.VMEM(shape, jnp.float32) for shape in shapes]
        + semaphores
        + column_sems(cols, 2)
        + stepped
        + [pltpu.VMEM(shape, jnp.float32) for shape in staged],
        compiler_params=pltpu.CompilerParams(collective_id=1, has_side_effects=True, vmem_limit_bytes=48 * 1024 * 1024),
    )(panels_t, trailing)
    return r_block, spread.transpose(2, 0, 1).reshape(total // rows, -1)


def plain(panels_t, trailing_t):
    panel = lax.all_gather(panels_t, "col", axis=0, tiled=True)
    gram_part = lax.psum_scatter(product(panels_t, panel.T), "row", scatter_dimension=0, tiled=True)
    gram = lax.all_gather(gram_part, ("col", "row"), axis=0, tiled=True)
    cross = lax.psum_scatter(product(trailing_t, panel.T), "row", scatter_dimension=0, tiled=True)
    r_full, invert = factor(gram)
    slab = product(product(cross, invert.T), invert)
    return r_full, lax.all_to_all(slab, "row", split_axis=1, concat_axis=0, tiled=True).T


def local(panels_t, trailing_t):
    rows, cols = lax.axis_size("row"), lax.axis_size("col")
    width = panels_t.shape[0]
    total = width * cols
    thick = trailing_t.shape[0] // rows
    tiled = width % BLOCK == 0 and total // rows % BLOCK == 0 and width // rows % (cols * MICRO) == 0 and thick % MICRO == 0
    if tiled and rows % 2 == 0 and cols % 2 == 0 and rows // 2 + LATE < total // BLOCK and cols >= 4 and rows % 4 == 0 and rows >= 8 and BLOCK % (rows * MICRO) == 0 and width == 2 * BLOCK:
        return direct(panels_t, trailing_t, rows, cols)
    r_full, coef_block = plain(panels_t, trailing_t)
    rows_out = total // rows
    row_start = lax.axis_index("row") * rows_out
    col_start = lax.axis_index("col") * width
    r_block = lax.dynamic_slice(r_full, (row_start, col_start), (rows_out, width))
    return (r_block, coef_block)


def solution(mesh):
    placed = (P("col", "row"), P("col", "row"))
    return jax.shard_map(
        local,
        mesh=mesh,
        in_specs=placed,
        out_specs=(P("row", "col"), P("row", "col")),
        check_vma=False,
    )
```
